256 devices in a mesh: leaf: 64 (over y, z, core), grid: 4 (over x).
Axes of the slice: x: 4, y: 4, z: 8, core: 2. Of those that a mesh axis runs over, the one named last changes fastest.
Arguments:
- rhs: bfloat16 [5, 128, 256, 256], P(None, 'leaf', 'grid'), may hold values from -6 to 6
- fwd_inv: bfloat16 [5, 128, 256, 256], P(None, 'leaf', 'grid')
- bwd_inv: bfloat16 [5, 128, 256, 256], P(None, 'leaf', 'grid')
- upd_t: bfloat16 [4, 128, 256, 512], P(None, 'leaf', 'grid'), may hold values from -0.25 to 0.25
- bwd_t: bfloat16 [4, 128, 512, 256], P(None, 'leaf', 'grid'), may hold values from -0.1875 to 0.1875
- dest_owner: int32 [4, 64, 4, 256, 1], P(None, 'leaf', 'grid'), may hold values from 0 to 63; in each aligned block of 256 rows (0 to 255, 256 to 511, ..., all dimensions but the last counted through in order) at most 10 rows name the same one
- dest_row: int32 [4, 64, 4, 256], P(None, 'leaf', 'grid'), may hold values from 128 to 639, as said below
Outputs:
- solution: bfloat16 [5, 128, 256, 256], P(None, 'leaf', 'grid')
The draws below stay inside these ranges and needn't reach their ends.
Inputs may be any that keep to these rules, and one draw needn't show every extreme that they name: `dest_owner`: in the rows of one device at one level (one aligned block of 256), no owner is named more than 10 times, a bound that some block reaches. `dest_row`: an entry of level l reaches a row of a later level: it lies from (l + 1) * 2 * 64 to 639.
All inputs are finite; a program needn't handle non-finite values.
Results may differ from the reference program's by a relative error of at most 0.025.
Values may be sent and summed in bfloat16 or wider, within the bound.
A program may use at most 64 MiB of HBM per device.

```python
import math
import jax
import jax.numpy as jnp
import numpy as np
from jax import lax

W = 256
NRHS = 256
R = 512
LEV = 5
K = 2
LEAVES = 64
GROUPS = 4
SUPER = 128
LEVM1 = 4
WG = 64
RG = 128
CAP = 10


def unit_blocks(key, salt):
    base_key = jax.random.fold_in(key, salt)
    identity_mat = (lax.broadcasted_iota(jnp.int32, (W, W), 0) == lax.broadcasted_iota(jnp.int32, (W, W), 1)).astype(jnp.float32)
    noise_part = jax.random.normal(base_key, (LEV, SUPER, W, W), jnp.float32) * (0.5 / math.sqrt(W))
    return (identity_mat + noise_part).astype(jnp.bfloat16)


def draw_fwd_inv(key, part):
    return unit_blocks(key, 11)


def draw_bwd_inv(key, part):
    return unit_blocks(key, 23)


def draw_dest_row(key, part):
    base_key = jax.random.fold_in(key, 37)
    lowest = ((jnp.arange(LEVM1, dtype=jnp.int32) + 1) * (K * WG)).reshape(LEVM1, 1, 1, 1)
    return jax.random.randint(base_key, (LEVM1, LEAVES, GROUPS, RG * K), lowest, LEV * K * WG, dtype=jnp.int32)


def levels(own_key, shape, shards, least, largest):
    def one(axis_at, blocks):
        steps = jax.random.uniform(jax.random.fold_in(jax.random.fold_in(own_key, 6), axis_at), (blocks,), jnp.float32, least / len(shards), largest / len(shards))
        return jnp.repeat(jnp.exp(steps), shape[axis_at] // blocks).reshape((-1,) + (1,) * (len(shape) - axis_at - 1))

    gain = one(*shards[0])
    for cut in shards[1:]:
        gain = gain * one(*cut)
    return gain


def shared_out(stream_key, own, number, rows, number_of, top, reach, lean):
    ranking = jax.random.permutation(stream_key, number_of)
    crowded, common = shares(number_of, rows * top, reach, lean, True), shares(number_of, rows * top, reach, lean, False)
    places = jnp.arange(number_of)

    def named(lengths, rotation):
        used = int((lengths > 0).sum())
        fixed = max(1, used // 4)
        passed = fixed + (places - fixed + rotation * (used - fixed)) % max(1, number_of - fixed)
        return jnp.zeros((number_of,), jnp.int32).at[ranking[jnp.where(places < fixed, places, passed)]].set(jnp.asarray(lengths, jnp.int32))

    lengths = jnp.where(number % 4 == 0, named(crowded, number // 4), named(common, number - number // 4 - 1))
    mixed = jax.random.permutation(jax.random.fold_in(own, 3), number_of)
    source_of, taker = mixed[0:number_of // 2 * 2:2], mixed[1:number_of // 2 * 2:2]
    margin = jnp.minimum(lengths[source_of] - 1, reach - lengths[taker]) // 2
    margin = jnp.where((source_of == ranking[0]) | (taker == ranking[0]) | (lengths[taker] == 0), 0, jnp.maximum(margin, 0))
    passed = jax.random.randint(jax.random.fold_in(own, 4), (number_of // 2,), 0, 1 << 20) % (margin + 1)
    lengths = lengths.at[source_of].add(-passed).at[taker].add(passed)
    items = jnp.searchsorted(jnp.cumsum(lengths), jnp.arange(rows * top), side="right").astype(jnp.int32)
    table = items.reshape(top, rows).T
    table = table[jax.random.permutation(jax.random.fold_in(own, 1), rows)]
    rotation = jax.random.randint(jax.random.fold_in(own, 2), (rows, 1), 0, top)
    return jnp.take_along_axis(table, (jnp.arange(top)[None, :] + rotation) % top, axis=1)


def shares(count, total, limit, slope, full):
    weights = [(1 << 20) // math.isqrt(grade ** slope) + 1 for grade in range(1, count + 1)]
    largest = limit if full else min(limit, max(-(-total // count), total * weights[0] // sum(weights)))
    least = 1 if total - largest >= count - 1 else 0
    given, rest = [largest] + [least] * (count - 1), total - largest - least * (count - 1)
    while rest > 0:
        candidates = [i for i in range(1, count) if given[i] < largest] or [i for i in range(1, count) if given[i] < limit]
        whole, budget = sum([weights[i] for i in candidates]), rest
        for i in candidates:
            more = min(limit - given[i], max(1, budget * weights[i] // whole), rest)
            given[i] = given[i] + more
            rest = rest - more
    return np.array(given)


def normal_values(key, dims, spread, reach, pieces=(), kind=jnp.bfloat16):
    array = jax.random.normal(key, dims, jnp.float32) * spread
    if len(pieces) > 0:
        array = levels(key, dims, pieces, -0.22, 0.18) * array
    return jnp.clip(array, min=-reach, max=reach).astype(kind)


def setup_inputs(seed: int = 0) -> dict:
    arg_keys = jax.random.split(jax.random.key(seed), 8)
    rhs = normal_values(arg_keys[0], (LEV, SUPER, W, NRHS), 1.0, 6.0, ((1, 64), (2, 4)))
    fwd_inv = draw_fwd_inv(jax.random.fold_in(arg_keys[7], 71), 0)
    bwd_inv = draw_bwd_inv(jax.random.fold_in(arg_keys[7], 71), 0)
    upd_t = normal_values(arg_keys[3], (LEVM1, SUPER, W, R), (2 * W) ** -0.5, 0.25, ((1, 64), (2, 4)))
    bwd_t = normal_values(arg_keys[4], (LEVM1, SUPER, R, W), (2 * R) ** -0.5, 0.1875, ((1, 64), (2, 4)))
    dest_owner_keys = jax.random.split(jax.random.fold_in(arg_keys[5], 1), LEVM1 * LEAVES * GROUPS * (RG * K) // (RG * K))
    dest_owner_turns = jax.random.permutation(jax.random.fold_in(arg_keys[5], 3), LEVM1 * LEAVES * GROUPS * (RG * K) // (RG * K))
    dest_owner = jax.vmap(lambda own, number: shared_out(jax.random.fold_in(arg_keys[5], 2), own, number, RG * K, LEAVES, 1, CAP, 2))(dest_owner_keys, dest_owner_turns).reshape((LEVM1, LEAVES, GROUPS, RG * K, 1))
    dest_row = draw_dest_row(jax.random.fold_in(arg_keys[7], 71), 0)
    return dict(rhs=rhs, fwd_inv=fwd_inv, bwd_inv=bwd_inv, upd_t=upd_t, bwd_t=bwd_t, dest_owner=dest_owner, dest_row=dest_row)


def widen(values):
    return lax.optimization_barrier(values).astype(jnp.float32)


def flat_targets(dest_owner, dest_row, level):
    owner_ids = dest_owner[level][..., 0]
    offsets = dest_row[level]
    group_ids = jnp.arange(GROUPS, dtype=jnp.int32)[None, :, None]
    level_to = offsets // (K * WG)
    super_to = owner_ids * K + (offsets // WG) % K
    row_to = group_ids * WG + offsets % WG
    return ((level_to * SUPER + super_to) * W + row_to).reshape(-1).astype(jnp.int32)


def to_routed(values):
    shaped = values.reshape(LEAVES, K, GROUPS, RG, NRHS)
    return jnp.transpose(shaped, (0, 2, 3, 1, 4)).reshape(-1, NRHS)


def from_routed(values):
    shaped = values.reshape(LEAVES, GROUPS, RG, K, NRHS)
    return jnp.transpose(shaped, (0, 3, 1, 2, 4)).reshape(SUPER, R, NRHS)


def reference(rhs, fwd_inv, bwd_inv, upd_t, bwd_t, dest_owner, dest_row):
    level_rows = SUPER * W
    accum = rhs.astype(jnp.float32).reshape(LEV * level_rows, NRHS)
    forward_out = []
    for level in range(LEV):
        block = accum[level * level_rows:(level + 1) * level_rows].reshape(SUPER, W, NRHS).astype(jnp.bfloat16)
        solved = jnp.einsum('swv,svn->swn', widen(fwd_inv[level]), widen(block))
        forward_out.append(solved)
        if level < LEV - 1:
            lowered = solved.astype(jnp.bfloat16)
            summed = jnp.zeros((SUPER, R, NRHS), jnp.float32)
            for group in range(GROUPS):
                lower_part = widen(upd_t[level][:, group * WG:(group + 1) * WG, :])
                term = jnp.einsum('swr,swn->srn', lower_part, widen(lowered[:, group * WG:(group + 1) * WG, :]))
                summed = summed + widen(term.astype(jnp.bfloat16))
            accum = accum.at[flat_targets(dest_owner, dest_row, level)].add(-to_routed(summed))
    solution = jnp.zeros((LEV * level_rows, NRHS), jnp.bfloat16)
    for level in reversed(range(LEV)):
        reduced = forward_out[level]
        if level < LEV - 1:
            pulled = from_routed(solution[flat_targets(dest_owner, dest_row, level)])
            for group in range(GROUPS):
                upper_rows = widen(bwd_t[level][:, group * RG:(group + 1) * RG, :])
                term = jnp.einsum('sjw,sjn->swn', upper_rows, widen(pulled[:, group * RG:(group + 1) * RG, :]))
                reduced = reduced - widen(term.astype(jnp.bfloat16))
        result = jnp.einsum('swv,svn->swn', widen(bwd_inv[level]), widen(reduced.astype(jnp.bfloat16)))
        solution = solution.at[level * level_rows:(level + 1) * level_rows].set(result.astype(jnp.bfloat16).reshape(level_rows, NRHS))
    return solution.reshape(LEV, SUPER, W, NRHS)
```

```python
import jax
import jax.numpy as jnp
from jax import lax
from jax.experimental import pallas as pl
from jax.experimental.pallas import tpu as pltpu
from jax.sharding import PartitionSpec as P

MESH = pl.DeviceIdType.MESH
BF = jnp.bfloat16
F32 = jnp.float32
LANES = 128


def dot(a, b):
    return jnp.dot(a, b, preferred_element_type=F32)


def dot_t(a, b):
    return lax.dot_general(a, b, (((0,), (0,)), ((), ())), preferred_element_type=F32)


def solve_kernel(
    sizes,
    rhs,
    fwd_inv,
    bwd_inv,
    upd,
    bwd,
    pos_r,
    pos_c,
    idx_r,
    idx_c,
    out,
    finv,
    binv,
    ucol,
    blk,
    low,
    acc,
    const,
    sol,
    sbuf,
    rbuf,
    rs_s,
    rs_r,
    pm,
    pt,
    sm,
    gm,
    fs,
    fr,
    us,
    ur,
    bs,
    br,
    ag_s,
    ag_r,
    aa_s,
    aa_r,
    rd_s,
    rd_r,
):
    levels, per, rows, group_rows, owners, groups, cap, halves = sizes
    sends = levels - 1
    width = rows * groups
    block = per * rows
    slots = owners * cap
    routed = per * group_rows
    me = lax.axis_index("leaf")
    gx = lax.axis_index("grid")
    my_rows = pl.ds(pl.multiple_of(gx * rows, rows), rows)
    others = owners - 1

    def peer(step):
        return lax.rem(gx + step, groups)

    def remote(src, dst, send, recv, leaf, grid):
        return pltpu.make_async_remote_copy(
            src_ref=src,
            dst_ref=dst,
            send_sem=send,
            recv_sem=recv,
            device_id=(leaf, grid),
            device_id_type=MESH,
        )

    barrier = pltpu.get_barrier_semaphore()

    def greet(i, c):
        pl.semaphore_signal(
            barrier, inc=1, device_id=(lax.rem(me + i, owners), gx), device_id_type=MESH
        )
        return c

    lax.fori_loop(1, owners, greet, 0)
    for step in range(1, groups):
        pl.semaphore_signal(barrier, inc=1, device_id=(me, peer(step)), device_id_type=MESH)
    pl.semaphore_wait(barrier, others + groups - 1)

    def part(ref, count):
        return ref.at[:, pl.ds(0, count), :]

    def matrix(level, ref, mine, send, recv):
        for step in range(1, groups):
            remote(
                mine.at[level],
                ref.at[level, :, my_rows, :],
                send.at[level],
                recv.at[level],
                me,
                peer(step),
            ).start()

    def matrix_sync(level, ref, send, recv, sent):
        view = part(ref.at[level], width - rows)
        copy = remote(view, view, send.at[level], recv.at[level], me, peer(1))
        copy.wait_send() if sent else copy.wait_recv()

    def columns(level):
        for step in range(1, groups):
            to = peer(step)
            remote(
                upd.at[level, :, :, pl.ds(pl.multiple_of(to * group_rows, group_rows), group_rows)],
                ucol.at[level, :, my_rows, :],
                us.at[level],
                ur.at[level],
                me,
                to,
            ).start()

    def gather(level, h):
        view = blk.at[level, h, :, my_rows, :]
        for step in range(1, groups):
            remote(view, view, ag_s.at[level, h], ag_r.at[level, h], me, peer(step)).start()

    def gather_sync(level, h, sent):
        view = part(blk.at[level, h], width - rows)
        copy = remote(view, view, ag_s.at[level, h], ag_r.at[level, h], me, peer(1))
        copy.wait_send() if sent else copy.wait_recv()

    def exchange(phase, h):
        def body(i, c):
            to = lax.rem(me + i, owners)
            remote(
                sbuf.at[phase, h, to],
                rbuf.at[phase, h, me],
                aa_s.at[phase, h],
                aa_r.at[phase, h],
                to,
                gx,
            ).start()
            return c

        lax.fori_loop(1, owners, body, 0)
        rbuf[phase, h, me] = sbuf[phase, h, me]

    def exchange_sync(phase, h, sent):
        view = (sbuf if sent else rbuf).at[phase, h, pl.ds(0, others)]
        to = lax.rem(me + 1, owners)
        copy = remote(view, view, aa_s.at[phase, h], aa_r.at[phase, h], to, gx)
        copy.wait_send() if sent else copy.wait_recv()

    def reduce_start(level, h):
        for step in range(1, groups):
            to = peer(step)
            remote(
                rs_s.at[level, h, :, pl.ds(pl.multiple_of(to * rows, rows), rows), :],
                rs_r.at[level, h, gx],
                rd_s.at[level, h],
                rd_r.at[level, h],
                me,
                to,
            ).start()

    def reduce_sync(level, h, sent):
        view = rs_r.at[level, h, pl.ds(0, groups - 1)]
        copy = remote(view, view, rd_s.at[level, h], rd_r.at[level, h], me, peer(1))
        copy.wait_send() if sent else copy.wait_recv()

    def hot(mask):
        return jnp.where(mask, 1.0, 0.0).astype(BF)

    def build_p(level):
        for c in range(slots // LANES):
            at = lax.broadcasted_iota(jnp.int32, (LANES, routed), 0) + c * LANES
            pm[level, pl.ds(c * LANES, LANES), :] = hot(at == pos_r[level])

    def build_pt(level):
        for c in range(routed // LANES):
            span = pl.ds(c * LANES, LANES)
            at = lax.broadcasted_iota(jnp.int32, (LANES, slots), 1)
            pt[level, span, :] = hot(at == pos_c[level, span, :])

    def build_s(level):
        for c in range(sends * block // LANES):
            at = lax.broadcasted_iota(jnp.int32, (LANES, slots), 0) + (c * LANES + block + 1)
            sm[level, pl.ds(c * LANES, LANES), :] = hot(at == idx_r[level])

    def build_g(level):
        for c in range(slots // LANES):
            span = pl.ds(c * LANES, LANES)
            at = lax.broadcasted_iota(jnp.int32, (LANES, sends * block), 1) + (block + 1)
            gm[level, span, :] = hot(at == idx_c[level, span, :])

    def pack(phase, h, value):
        sbuf[phase, h] = value.astype(BF).reshape(owners, cap // 2, 2, LANES)

    def unpack(phase, h):
        return rbuf[phase, h].reshape(slots, LANES)

    for h in range(halves):
        blk[0, h, :, my_rows, :] = rhs[0, :, :, h * LANES : (h + 1) * LANES]
        gather(0, h)
    matrix(0, finv, fwd_inv, fs, fr)
    columns(0)
    my_columns = pl.ds(pl.multiple_of(gx * group_rows, group_rows), group_rows)
    for level in range(levels):
        finv[level, :, my_rows, :] = fwd_inv[level]
        if level < sends:
            binv[level, :, my_rows, :] = bwd_inv[level]
            ucol[level, :, my_rows, :] = upd[level, :, :, my_columns]
        if level > 0:
            for h in range(halves):
                acc[level, h] = (
                    rhs[level, :, :, h * LANES : (h + 1) * LANES].astype(F32).reshape(block, LANES)
                )
    for level in range(sends):
        build_p(level)

    def lower(level, h):
        matrix_waited = []
        for k in range(per):
            solved = dot(finv[level, k], blk[level, h, k])
            low[h, k] = solved.astype(BF)
            matrix_waited.append(low[h, k])
        return matrix_waited

    def forward(level, c):
        matrix_sync(level, finv, fs, fr, False)
        view = part(ucol.at[level], width - rows)
        remote(view, view, us.at[level], ur.at[level], me, peer(1)).wait_recv()
        for h in range(halves):
            gather_sync(level, h, False)
            lowered = lower(level, h)
            summed = [dot_t(ucol[level, k], lowered[k]).astype(BF) for k in range(per)]
            packed = dot(pm[level], jnp.concatenate(summed, axis=0))
            pack(level, h, packed)
            exchange(level, h)
        matrix(level + 1, finv, fwd_inv, fs, fr)

        @pl.when(level < sends - 1)
        def _():
            columns(level + 1)

        @pl.when(level == sends - 1)
        def _():
            matrix(sends - 1, binv, bwd_inv, bs, br)

        build_s(level)
        build_g(level)
        build_pt(level)
        for h in range(halves):
            for k in range(per):
                const[level, h, k] = dot(bwd_inv[level, k], low[h, k])
        for h in range(halves):
            exchange_sync(level, h, False)
            come = unpack(level, h)
            chosen = sm[level, pl.ds(pl.multiple_of(level * block, block), block), :]
            total = acc[level + 1, h] - dot(chosen, come)
            blk[level + 1, h, :, my_rows, :] = total.astype(BF).reshape(per, rows, LANES)
            gather(level + 1, h)
        for h in range(halves):
            come = unpack(level, h)

            def later(target, c, h=h, come=come):
                span = pl.ds(pl.multiple_of((target - 1) * block, block), block)
                acc[target, h] = acc[target, h] - dot(sm[level, span, :], come)
                return c

            lax.fori_loop(level + 2, levels, later, 0)
        return c

    lax.fori_loop(0, sends, forward, 0)

    def finish(level, h, k, value):
        result = value.astype(BF)
        at = level * block + k * rows
        if not isinstance(at, int):
            at = pl.multiple_of(at, rows)
        sol[h, pl.ds(at, rows), :] = result
        out[level, k, :, h * LANES : (h + 1) * LANES] = result

    sol[...] = jnp.zeros(sol.shape, BF)
    matrix_sync(sends, finv, fs, fr, False)
    for h in range(halves):
        gather_sync(sends, h, False)
        lowered = lower(sends, h)
        for k in range(per):
            finish(sends, h, k, dot(bwd_inv[sends, k], lowered[k]))

    def backward(i, c):
        level = sends - 1 - i
        phase = sends + level
        for h in range(halves):
            answer = dot(gm[level], sol[h, pl.ds(block, sends * block), :])
            pack(phase, h, answer)
            exchange(phase, h)

        @pl.when(level > 0)
        def _():
            matrix(level - 1, binv, bwd_inv, bs, br)

        matrix_sync(level, binv, bs, br, False)
        for h in range(halves):
            exchange_sync(phase, h, False)
            pulled = dot(pt[level], unpack(phase, h)).astype(BF)
            for k in range(per):
                upper = dot_t(bwd[level, k], pulled[k * group_rows : (k + 1) * group_rows])
                rs_s[level, h, k] = dot(binv[level, k], upper.astype(BF)).astype(BF)
            reduce_start(level, h)
        for h in range(halves):
            reduce_sync(level, h, False)
            for k in range(per):
                total = rs_s[level, h, k, my_rows, :].astype(F32)
                for step in range(1, groups):
                    total = total + rs_r[level, h, peer(step), k].astype(F32)
                finish(level, h, k, const[level, h, k] - total)
        return c

    lax.fori_loop(0, sends, backward, 0)

    def drain(level, c):
        matrix_sync(level, finv, fs, fr, True)
        for h in range(halves):
            gather_sync(level, h, True)
        return c

    lax.fori_loop(0, levels, drain, 0)

    def drain_sends(level, c):
        matrix_sync(level, binv, bs, br, True)
        view = part(ucol.at[level], width - rows)
        remote(view, view, us.at[level], ur.at[level], me, peer(1)).wait_send()
        for h in range(halves):
            exchange_sync(level, h, True)
            exchange_sync(level + sends, h, True)
            reduce_sync(level, h, True)
        return c

    lax.fori_loop(0, sends, drain_sends, 0)


def local(rhs, fwd_inv, bwd_inv, upd_t, bwd_t, dest_owner, dest_row):
    levels, per, rows, cols = rhs.shape
    group_rows = bwd_t.shape[2]
    owners = lax.axis_size("leaf")
    groups = lax.axis_size("grid")
    cap = max(2, 8 * per * group_rows // (3 * owners))
    sends = levels - 1
    halves = cols // LANES
    slots = owners * cap
    routed = per * group_rows
    block = per * rows
    width = rows * groups

    def by_supernode(index):
        split = index.reshape(sends, group_rows, per)
        return jnp.swapaxes(split, 1, 2).reshape(sends, routed)

    owner = by_supernode(dest_owner)
    target = by_supernode(dest_row)
    order = jnp.arange(routed, dtype=jnp.int32)
    same = (owner[:, :, None] == owner[:, None, :]) & (order[None, None, :] < order[None, :, None])
    position = owner * cap + jnp.sum(same.astype(jnp.int32), axis=2)
    slot_ids = jnp.arange(slots, dtype=jnp.int32)
    chosen = slot_ids[None, :, None] == position[:, None, :]
    asked = jnp.sum(jnp.where(chosen, target[:, None, :] + 1, 0), axis=2)
    asked = jnp.swapaxes(asked.reshape(sends, owners, cap), 0, 1).reshape(owners, sends * cap)
    told = lax.all_to_all(asked, "leaf", split_axis=0, concat_axis=0, tiled=True)
    told = jnp.swapaxes(told.reshape(owners, sends, cap), 0, 1).reshape(sends, slots)

    dma = pltpu.SemaphoreType.DMA
    vmem = pltpu.VMEM
    sizes = (levels, per, rows, group_rows, owners, groups, cap, halves)

    def body(*refs):
        solve_kernel(sizes, *refs)

    return pl.pallas_call(
        body,
        out_shape=jax.ShapeDtypeStruct(rhs.shape, BF),
        in_specs=[pl.BlockSpec(memory_space=vmem)] * 9,
        out_specs=pl.BlockSpec(memory_space=vmem),
        scratch_shapes=[
            vmem((levels, per, width, width), BF),
            vmem((sends, per, width, width), BF),
            vmem((sends, per, width, group_rows), BF),
            vmem((levels, halves, per, width, LANES), BF),
            vmem((halves, per, width, LANES), BF),
            vmem((levels, halves, block, LANES), F32),
            vmem((sends, halves, per, rows, LANES), F32),
            vmem((halves, levels * block, LANES), BF),
            vmem((2 * sends, halves, owners, cap // 2, 2, LANES), BF),
            vmem((2 * sends, halves, owners, cap // 2, 2, LANES), BF),
            vmem((sends, halves, per, width, LANES), BF),
            vmem((sends, halves, groups, per, rows, LANES), BF),
            vmem((sends, slots, routed), BF),
            vmem((sends, routed, slots), BF),
            vmem((sends, sends * block, slots), BF),
            vmem((sends, slots, sends * block), BF),
            dma((levels,)),
            dma((levels,)),
            dma((sends,)),
            dma((sends,)),
            dma((sends,)),
            dma((sends,)),
            dma((levels, halves)),
            dma((levels, halves)),
            dma((2 * sends, halves)),
            dma((2 * sends, halves)),
            dma((sends, halves)),
            dma((sends, halves)),
        ],
        compiler_params=pltpu.CompilerParams(collective_id=0, has_side_effects=True),
    )(
        rhs,
        fwd_inv,
        bwd_inv,
        upd_t,
        bwd_t,
        position[:, None, :],
        position[:, :, None],
        told[:, None, :],
        told[:, :, None],
    )


def solution(mesh):
    placed = (
        P(None, "leaf", "grid", None),
        P(None, "leaf", "grid", None),
        P(None, "leaf", "grid", None),
        P(None, "leaf", "grid", None),
        P(None, "leaf", "grid", None),
        P(None, "leaf", "grid", None, None),
        P(None, "leaf", "grid", None),
    )
    return jax.shard_map(
        local, mesh=mesh, in_specs=placed, out_specs=P(None, "leaf", "grid", None), check_vma=False
    )
```

```python
import jax
import jax.numpy as jnp
from jax import lax
from jax.experimental import pallas as pl
from jax.experimental.pallas import tpu as pltpu
from jax.sharding import PartitionSpec as P

MESH = pl.DeviceIdType.MESH
BF = jnp.bfloat16
F32 = jnp.float32
LANES = 128
RING_Y, RING_Z, CORES = 4, 8, 2
SLOT_LANES = 16


def dot(a, b):
    return jnp.dot(a, b, preferred_element_type=F32)


def dot_t(a, b):
    return lax.dot_general(a, b, (((0,), (0,)), ((), ())), preferred_element_type=F32)


def count_out(place, count):
    return count // 2 + (place + 1) // 2 * (1 - 2 * (place % 2))


def solve_kernel(
    sizes,
    rhs,
    fwd_inv,
    bwd_inv,
    upd,
    bwd,
    own_r,
    own_c,
    want_r,
    out,
    finv,
    binv,
    ucol,
    blk,
    low,
    acc,
    const,
    sol,
    sbuf,
    rbuf,
    rs_s,
    rs_r,
    pm,
    pt,
    sm,
    gm,
    told,
    by_row,
    by_col,
    asked,
    pick,
    pos_r,
    pos_c,
    fs,
    fr,
    us,
    ur,
    bs,
    br,
    ag_s,
    ag_r,
    aa_s,
    aa_r,
    rd_s,
    rd_r,
    ix_s,
    ix_r,
):
    levels, per, rows, group_rows, owners, groups, cap, halves = sizes
    sends = levels - 1
    width = rows * groups
    block = per * rows
    slots = owners * cap
    routed = per * group_rows
    me = lax.axis_index("leaf")
    gx = lax.axis_index("grid")
    my_rows = pl.ds(pl.multiple_of(gx * rows, rows), rows)
    others = owners - 1
    my_y = lax.div(me, RING_Z * CORES)
    my_z = lax.rem(lax.div(me, CORES), RING_Z)
    my_core = lax.rem(me, CORES)

    def peer(step):
        return lax.rem(gx + step, groups)

    def outward(place, count):
        half = lax.div(place + 1, 2)
        return count // 2 + half * (1 - 2 * lax.rem(place, 2))

    ring = [
        lax.rem(my_z + count_out(a, RING_Z), RING_Z) * CORES for a in range(RING_Z)
    ]

    def each_partner(act):
        def group(j, last):
            y = lax.rem(my_y + outward(lax.rem(j, RING_Y), RING_Y), RING_Y)
            core = lax.rem(my_core + 1 - lax.div(j, RING_Y), CORES)
            base = y * (RING_Z * CORES) + core
            for a in range(RING_Z - last):
                act(base + ring[a])

        def body(j, c):
            group(j, 0)
            return c

        lax.fori_loop(0, RING_Y * CORES - 1, body, 0)
        group(jnp.int32(RING_Y * CORES - 1), 1)

    def remote(src, dst, send, recv, leaf, grid):
        return pltpu.make_async_remote_copy(
            src_ref=src,
            dst_ref=dst,
            send_sem=send,
            recv_sem=recv,
            device_id=(leaf, grid),
            device_id_type=MESH,
        )

    barrier = pltpu.get_barrier_semaphore()

    def greet(to):
        pl.semaphore_signal(barrier, inc=1, device_id=(to, gx), device_id_type=MESH)

    each_partner(greet)
    for step in range(1, groups):
        pl.semaphore_signal(barrier, inc=1, device_id=(me, peer(step)), device_id_type=MESH)

    def part(ref, count):
        return ref.at[:, pl.ds(0, count), :]

    def matrix(level, ref, mine, send, recv):
        for step in range(1, groups):
            remote(
                mine.at[level],
                ref.at[level, :, my_rows, :],
                send.at[level],
                recv.at[level],
                me,
                peer(step),
            ).start()

    def matrix_sync(level, ref, send, recv, sent):
        view = part(ref.at[level], width - rows)
        copy = remote(view, view, send.at[level], recv.at[level], me, peer(1))
        copy.wait_send() if sent else copy.wait_recv()

    def columns(level):
        for step in range(1, groups):
            to = peer(step)
            remote(
                upd.at[level, :, :, pl.ds(pl.multiple_of(to * group_rows, group_rows), group_rows)],
                ucol.at[level, :, my_rows, :],
                us.at[level],
                ur.at[level],
                me,
                to,
            ).start()

    def gather(level, h):
        view = blk.at[level, h, :, my_rows, :]
        for step in range(1, groups):
            remote(view, view, ag_s.at[level, h], ag_r.at[level, h], me, peer(step)).start()

    def gather_sync(level, h, sent):
        view = part(blk.at[level, h], width - rows)
        copy = remote(view, view, ag_s.at[level, h], ag_r.at[level, h], me, peer(1))
        copy.wait_send() if sent else copy.wait_recv()

    def exchange(phase, h):
        def send(to):
            remote(
                sbuf.at[phase, h, to],
                rbuf.at[phase, h, me],
                aa_s.at[phase, h],
                aa_r.at[phase, h],
                to,
                gx,
            ).start()

        each_partner(send)
        rbuf[phase, h, me] = sbuf[phase, h, me]

    def exchange_sync(phase, h, sent):
        view = (sbuf if sent else rbuf).at[phase, h, pl.ds(0, others)]
        to = lax.rem(me + 1, owners)
        copy = remote(view, view, aa_s.at[phase, h], aa_r.at[phase, h], to, gx)
        copy.wait_send() if sent else copy.wait_recv()

    def reduce_start(level, h):
        for step in range(1, groups):
            to = peer(step)
            remote(
                rs_s.at[level, h, :, pl.ds(pl.multiple_of(to * rows, rows), rows), :],
                rs_r.at[level, h, gx],
                rd_s.at[level, h],
                rd_r.at[level, h],
                me,
                to,
            ).start()

    def reduce_sync(level, h, sent):
        view = rs_r.at[level, h, pl.ds(0, groups - 1)]
        copy = remote(view, view, rd_s.at[level, h], rd_r.at[level, h], me, peer(1))
        copy.wait_send() if sent else copy.wait_recv()

    def hot(mask):
        return jnp.where(mask, 1.0, 0.0).astype(BF)

    def index_level(level):
        row, column, want = own_r[level], own_c[level], want_r[level]
        down = lax.broadcasted_iota(jnp.int32, (routed, routed), 0)
        across = lax.broadcasted_iota(jnp.int32, (routed, routed), 1)
        same = row == column
        rank_c = jnp.sum(jnp.where(same & (across < down), 1.0, 0.0), axis=1, keepdims=True)
        rank_r = jnp.sum(jnp.where(same & (down < across), 1.0, 0.0), axis=0, keepdims=True)
        rank_c, rank_r = rank_c.astype(jnp.int32), rank_r.astype(jnp.int32)
        pos_r[level] = row * cap + rank_r
        pos_c[level] = column * cap + rank_c
        owner = lax.broadcasted_iota(jnp.int32, (owners, routed), 0)
        high = lax.div(want, 32)
        low_bits = (want - high * 32).astype(F32)
        high = jnp.where(owner == row, high.astype(F32), 0.0).astype(BF)
        low_bits = jnp.where(owner == row, low_bits, 0.0).astype(BF)
        lane = lax.broadcasted_iota(jnp.int32, (routed, LANES), 1)
        place = hot(lane == rank_c + level * SLOT_LANES)
        chosen = dot(high, place) * 32.0 + dot(low_bits, place)
        pick[...] = chosen if level == 0 else pick[...] + chosen

    def build_p(level):
        for c in range(slots // LANES):
            at = lax.broadcasted_iota(jnp.int32, (LANES, routed), 0) + c * LANES
            pm[level, pl.ds(c * LANES, LANES), :] = hot(at == pos_r[level])

    def build_pt(level):
        for c in range(routed // LANES):
            span = pl.ds(c * LANES, LANES)
            at = lax.broadcasted_iota(jnp.int32, (LANES, slots), 1)
            pt[level, span, :] = hot(at == pos_c[level, span, :])

    def build_s(level):
        at = lax.broadcasted_iota(jnp.int32, (SLOT_LANES, slots), 0)
        span = pl.ds(pl.multiple_of(level * SLOT_LANES, SLOT_LANES), SLOT_LANES)
        lane = lax.broadcasted_iota(jnp.int32, (1, slots), 1)
        own = lane - lax.div(lane, cap) * cap
        row = jnp.sum(jnp.where(at == own, by_row[span, :], 0.0), axis=0, keepdims=True)
        row = row.astype(jnp.int32)
        for c in range(sends * block // LANES):
            at = lax.broadcasted_iota(jnp.int32, (LANES, slots), 0) + (c * LANES + block + 1)
            sm[level, pl.ds(c * LANES, LANES), :] = hot(at == row)

    def build_g(level):
        for c in range(slots // LANES):
            span = pl.ds(c * LANES, LANES)
            lane = lax.broadcasted_iota(jnp.int32, (LANES, LANES), 1)
            order = lax.broadcasted_iota(jnp.int32, (LANES, 1), 0) + c * LANES
            own = order - lax.div(order, cap) * cap + level * SLOT_LANES
            column = jnp.sum(jnp.where(lane == own, by_col[span, :], 0.0), axis=1, keepdims=True)
            at = lax.broadcasted_iota(jnp.int32, (LANES, sends * block), 1) + (block + 1)
            gm[level, span, :] = hot(at == column.astype(jnp.int32))

    def spread():
        number = told[...].reshape(owners, LANES)
        high = lax.div(number, 32)
        low_bits = (number - high * 32).astype(F32).astype(BF)
        high = high.astype(F32).astype(BF)
        first = lax.broadcasted_iota(jnp.int32, (slots, owners), 0)
        owner = lax.broadcasted_iota(jnp.int32, (slots, owners), 1) * cap
        fan = hot((first >= owner) & (first < owner + cap))
        by_col[...] = dot(fan, high) * 32.0 + dot(fan, low_bits)
        first = lax.broadcasted_iota(jnp.int32, (owners, slots), 1)
        owner = lax.broadcasted_iota(jnp.int32, (owners, slots), 0) * cap
        fan = hot((first >= owner) & (first < owner + cap))
        by_row[...] = dot_t(high, fan) * 32.0 + dot_t(low_bits, fan)

    def pack(phase, h, value):
        sbuf[phase, h] = value.astype(BF).reshape(owners, cap // 2, 2, LANES)

    def unpack(phase, h):
        return rbuf[phase, h].reshape(slots, LANES)

    for h in range(halves):
        blk[0, h, :, my_rows, :] = rhs[0, :, :, h * LANES : (h + 1) * LANES]
    pl.semaphore_wait(barrier, others + groups - 1)
    for h in range(halves):
        gather(0, h)
    matrix(0, finv, fwd_inv, fs, fr)
    columns(0)

    for level in range(sends):
        index_level(level)
    asked[...] = pick[...].astype(jnp.int32).reshape(owners, 1, LANES)

    def tell(to):
        remote(asked.at[to], told.at[me], ix_s, ix_r, to, gx).start()

    each_partner(tell)
    told[me] = asked[me]
    my_columns = pl.ds(pl.multiple_of(gx * group_rows, group_rows), group_rows)
    for level in range(levels):
        finv[level, :, my_rows, :] = fwd_inv[level]
        if level < sends:
            binv[level, :, my_rows, :] = bwd_inv[level]
            ucol[level, :, my_rows, :] = upd[level, :, :, my_columns]
        if level > 0:
            for h in range(halves):
                acc[level, h] = (
                    rhs[level, :, :, h * LANES : (h + 1) * LANES].astype(F32).reshape(block, LANES)
                )
    for level in range(sends):
        build_p(level)
    first = told.at[pl.ds(0, others)]
    remote(first, first, ix_s, ix_r, lax.rem(me + 1, owners), gx).wait_recv()
    spread()

    def lower(level, h):
        matrix_waited = []
        for k in range(per):
            solved = dot(finv[level, k], blk[level, h, k])
            low[h, k] = solved.astype(BF)
            matrix_waited.append(low[h, k])
        return matrix_waited

    def forward(level, c):
        matrix_sync(level, finv, fs, fr, False)
        view = part(ucol.at[level], width - rows)
        remote(view, view, us.at[level], ur.at[level], me, peer(1)).wait_recv()
        for h in range(halves):
            gather_sync(level, h, False)
            lowered = lower(level, h)
            summed = [dot_t(ucol[level, k], lowered[k]).astype(BF) for k in range(per)]
            packed = dot(pm[level], jnp.concatenate(summed, axis=0))
            pack(level, h, packed)
            exchange(level, h)
        matrix(level + 1, finv, fwd_inv, fs, fr)

        @pl.when(level < sends - 1)
        def _():
            columns(level + 1)

        @pl.when(level == sends - 1)
        def _():
            matrix(sends - 1, binv, bwd_inv, bs, br)

        build_s(level)
        build_g(level)
        build_pt(level)
        for h in range(halves):
            for k in range(per):
                const[level, h, k] = dot(bwd_inv[level, k], low[h, k])
        for h in range(halves):
            exchange_sync(level, h, False)
            come = unpack(level, h)
            chosen = sm[level, pl.ds(pl.multiple_of(level * block, block), block), :]
            total = acc[level + 1, h] - dot(chosen, come)
            blk[level + 1, h, :, my_rows, :] = total.astype(BF).reshape(per, rows, LANES)
            gather(level + 1, h)
        for h in range(halves):
            come = unpack(level, h)

            def later(target, c, h=h, come=come):
                span = pl.ds(pl.multiple_of((target - 1) * block, block), block)
                acc[target, h] = acc[target, h] - dot(sm[level, span, :], come)
                return c

            lax.fori_loop(level + 2, levels, later, 0)
        return c

    lax.fori_loop(0, sends, forward, 0)

    def finish(level, h, k, value):
        result = value.astype(BF)
        at = level * block + k * rows
        if not isinstance(at, int):
            at = pl.multiple_of(at, rows)
        sol[h, pl.ds(at, rows), :] = result
        out[level, k, :, h * LANES : (h + 1) * LANES] = result

    sol[...] = jnp.zeros(sol.shape, BF)
    matrix_sync(sends, finv, fs, fr, False)
    for h in range(halves):
        gather_sync(sends, h, False)
        lowered = lower(sends, h)
        for k in range(per):
            finish(sends, h, k, dot(bwd_inv[sends, k], lowered[k]))

    def backward(i, c):
        level = sends - 1 - i
        phase = sends + level
        for h in range(halves):
            answer = dot(gm[level], sol[h, pl.ds(block, sends * block), :])
            pack(phase, h, answer)
            exchange(phase, h)

        @pl.when(level > 0)
        def _():
            matrix(level - 1, binv, bwd_inv, bs, br)

        matrix_sync(level, binv, bs, br, False)
        for h in range(halves):
            exchange_sync(phase, h, False)
            pulled = dot(pt[level], unpack(phase, h)).astype(BF)
            for k in range(per):
                upper = dot_t(bwd[level, k], pulled[k * group_rows : (k + 1) * group_rows])
                rs_s[level, h, k] = dot(binv[level, k], upper.astype(BF)).astype(BF)
            reduce_start(level, h)
        for h in range(halves):
            reduce_sync(level, h, False)
            for k in range(per):
                total = rs_s[level, h, k, my_rows, :].astype(F32)
                for step in range(1, groups):
                    total = total + rs_r[level, h, peer(step), k].astype(F32)
                finish(level, h, k, const[level, h, k] - total)
        return c

    lax.fori_loop(0, sends, backward, 0)

    def drain(level, c):
        matrix_sync(level, finv, fs, fr, True)
        for h in range(halves):
            gather_sync(level, h, True)
        return c

    lax.fori_loop(0, levels, drain, 0)
    remote(first, first, ix_s, ix_r, lax.rem(me + 1, owners), gx).wait_send()

    def drain_sends(level, c):
        matrix_sync(level, binv, bs, br, True)
        view = part(ucol.at[level], width - rows)
        remote(view, view, us.at[level], ur.at[level], me, peer(1)).wait_send()
        for h in range(halves):
            exchange_sync(level, h, True)
            exchange_sync(level + sends, h, True)
            reduce_sync(level, h, True)
        return c

    lax.fori_loop(0, sends, drain_sends, 0)


def local(rhs, fwd_inv, bwd_inv, upd_t, bwd_t, dest_owner, dest_row):
    levels, per, rows, cols = rhs.shape
    group_rows = bwd_t.shape[2]
    owners = lax.axis_size("leaf")
    groups = lax.axis_size("grid")
    cap = max(2, 8 * per * group_rows // (3 * owners))
    sends = levels - 1
    halves = cols // LANES
    slots = owners * cap
    routed = per * group_rows
    block = per * rows
    width = rows * groups

    def by_supernode(index):
        split = index.reshape(sends, group_rows, per)
        return jnp.swapaxes(split, 1, 2).reshape(sends, routed)

    owner = by_supernode(dest_owner)
    target = by_supernode(dest_row)
    dma = pltpu.SemaphoreType.DMA
    vmem = pltpu.VMEM
    sizes = (levels, per, rows, group_rows, owners, groups, cap, halves)

    def body(*refs):
        solve_kernel(sizes, *refs)

    return pl.pallas_call(
        body,
        out_shape=jax.ShapeDtypeStruct(rhs.shape, BF),
        in_specs=[pl.BlockSpec(memory_space=vmem)] * 8,
        out_specs=pl.BlockSpec(memory_space=vmem),
        scratch_shapes=[
            vmem((levels, per, width, width), BF),
            vmem((sends, per, width, width), BF),
            vmem((sends, per, width, group_rows), BF),
            vmem((levels, halves, per, width, LANES), BF),
            vmem((halves, per, width, LANES), BF),
            vmem((levels, halves, block, LANES), F32),
            vmem((sends, halves, per, rows, LANES), F32),
            vmem((halves, levels * block, LANES), BF),
            vmem((2 * sends, halves, owners, cap // 2, 2, LANES), BF),
            vmem((2 * sends, halves, owners, cap // 2, 2, LANES), BF),
            vmem((sends, halves, per, width, LANES), BF),
            vmem((sends, halves, groups, per, rows, LANES), BF),
            vmem((sends, slots, routed), BF),
            vmem((sends, routed, slots), BF),
            vmem((sends, sends * block, slots), BF),
            vmem((sends, slots, sends * block), BF),
            vmem((owners, 1, LANES), jnp.int32),
            vmem((LANES, slots), F32),
            vmem((slots, LANES), F32),
            vmem((owners, 1, LANES), jnp.int32),
            vmem((owners, LANES), F32),
            vmem((sends, 1, routed), jnp.int32),
            vmem((sends, routed, 1), jnp.int32),
            dma((levels,)),
            dma((levels,)),
            dma((sends,)),
            dma((sends,)),
            dma((sends,)),
            dma((sends,)),
            dma((levels, halves)),
            dma((levels, halves)),
            dma((2 * sends, halves)),
            dma((2 * sends, halves)),
            dma((sends, halves)),
            dma((sends, halves)),
            dma,
            dma,
        ],
        compiler_params=pltpu.CompilerParams(collective_id=0, has_side_effects=True),
    )(
        rhs,
        fwd_inv,
        bwd_inv,
        upd_t,
        bwd_t,
        owner[:, None, :],
        owner[:, :, None],
        target[:, None, :] + 1,
    )


def solution(mesh):
    placed = (
        P(None, "leaf", "grid", None),
        P(None, "leaf", "grid", None),
        P(None, "leaf", "grid", None),
        P(None, "leaf", "grid", None),
        P(None, "leaf", "grid", None),
        P(None, "leaf", "grid", None, None),
        P(None, "leaf", "grid", None),
    )
    return jax.shard_map(
        local, mesh=mesh, in_specs=placed, out_specs=P(None, "leaf", "grid", None), check_vma=False
    )
```

```python
import jax
import jax.numpy as jnp
from jax import lax
from jax.experimental import pallas as pl
from jax.experimental.pallas import tpu as pltpu
from jax.sharding import PartitionSpec as P

MESH = pl.DeviceIdType.MESH
BF = jnp.bfloat16
F32 = jnp.float32
LANES = 128
RING_Y, RING_Z, CORES = 4, 8, 2
SLOT_LANES = 16
FAR_FIRST = (2, 1, 3)


def dot(a, b):
    return jnp.dot(a, b, preferred_element_type=F32)


def dot_t(a, b):
    return lax.dot_general(a, b, (((0,), (0,)), ((), ())), preferred_element_type=F32)


def count_out(place, count):
    return count // 2 + (place + 1) // 2 * (1 - 2 * (place % 2))


def solve_kernel(
    sizes,
    rhs_in,
    fwd_inv,
    bwd_in,
    upd,
    bwd_far,
    owner_in,
    target_in,
    out_far,
    finv,
    binv,
    ucol,
    blk,
    low,
    acc,
    const,
    sol,
    sbuf,
    rbuf,
    rs_s,
    rs_r,
    pm,
    pt,
    sm,
    gm,
    told,
    by_row,
    by_col,
    asked,
    pick,
    pos_r,
    pos_c,
    fs,
    fr,
    us,
    ur,
    bs,
    br,
    ag_s,
    ag_r,
    aa_s,
    aa_r,
    rd_s,
    rd_r,
    ix_s,
    ix_r,
    rhs,
    bwd_inv,
    bwd,
    out,
    in_sem,
    out_sem,
):
    levels, per, rows, group_rows, owners, groups, cap, halves = sizes
    sends = levels - 1
    width = rows * groups
    block = per * rows
    slots = owners * cap
    routed = per * group_rows
    me = lax.axis_index("leaf")
    gx = lax.axis_index("grid")
    my_rows = pl.ds(pl.multiple_of(gx * rows, rows), rows)
    others = owners - 1
    my_y = lax.div(me, RING_Z * CORES)
    my_z = lax.rem(lax.div(me, CORES), RING_Z)
    my_core = lax.rem(me, CORES)

    def peer(step):
        return lax.rem(gx + step, groups)

    def outward(place, count):
        half = lax.div(place + 1, 2)
        return count // 2 + half * (1 - 2 * lax.rem(place, 2))

    ring = [
        lax.rem(my_z + count_out(a, RING_Z), RING_Z) * CORES for a in range(RING_Z)
    ]

    def each_partner(act):
        def group(j, last):
            y = lax.rem(my_y + outward(lax.rem(j, RING_Y), RING_Y), RING_Y)
            core = lax.rem(my_core + 1 - lax.div(j, RING_Y), CORES)
            base = y * (RING_Z * CORES) + core
            for a in range(RING_Z - last):
                act(base + ring[a])

        def body(j, c):
            group(j, 0)
            return c

        lax.fori_loop(0, RING_Y * CORES - 1, body, 0)
        group(jnp.int32(RING_Y * CORES - 1), 1)

    def remote(src, dst, send, recv, leaf, grid):
        return pltpu.make_async_remote_copy(
            src_ref=src,
            dst_ref=dst,
            send_sem=send,
            recv_sem=recv,
            device_id=(leaf, grid),
            device_id_type=MESH,
        )

    barrier = pltpu.get_barrier_semaphore()

    def greet(to):
        pl.semaphore_signal(barrier, inc=1, device_id=(to, gx), device_id_type=MESH)

    each_partner(greet)
    for step in range(1, groups):
        pl.semaphore_signal(barrier, inc=1, device_id=(me, peer(step)), device_id_type=MESH)

    my_columns = pl.ds(pl.multiple_of(gx * group_rows, group_rows), group_rows)
    loads = [
        pltpu.make_async_copy(rhs_in, rhs, in_sem.at[0]),
        pltpu.make_async_copy(bwd_in, bwd_inv, in_sem.at[1]),
        pltpu.make_async_copy(bwd_far, bwd, in_sem.at[2]),
        pltpu.make_async_copy(fwd_inv, finv.at[:, :, my_rows, :], in_sem.at[3]),
        pltpu.make_async_copy(
            bwd_in.at[pl.ds(0, sends)], binv.at[:, :, my_rows, :], in_sem.at[4]
        ),
        pltpu.make_async_copy(
            upd.at[:, :, :, my_columns], ucol.at[:, :, my_rows, :], in_sem.at[5]
        ),
    ]
    for load in loads:
        load.start()

    def part(ref, count):
        return ref.at[:, pl.ds(0, count), :]

    def matrix(level, ref, mine, send, recv):
        for step in FAR_FIRST:
            remote(
                mine.at[level],
                ref.at[level, :, my_rows, :],
                send.at[level],
                recv.at[level],
                me,
                peer(step),
            ).start()

    def matrix_sync(level, ref, send, recv, sent):
        view = part(ref.at[level], width - rows)
        copy = remote(view, view, send.at[level], recv.at[level], me, peer(1))
        copy.wait_send() if sent else copy.wait_recv()

    def columns(level):
        for step in FAR_FIRST:
            to = peer(step)
            remote(
                upd.at[level, :, :, pl.ds(pl.multiple_of(to * group_rows, group_rows), group_rows)],
                ucol.at[level, :, my_rows, :],
                us.at[level],
                ur.at[level],
                me,
                to,
            ).start()

    def gather(level, h):
        view = blk.at[level, h, :, my_rows, :]
        for step in FAR_FIRST:
            remote(view, view, ag_s.at[level, h], ag_r.at[level, h], me, peer(step)).start()

    def gather_sync(level, h, sent):
        view = part(blk.at[level, h], width - rows)
        copy = remote(view, view, ag_s.at[level, h], ag_r.at[level, h], me, peer(1))
        copy.wait_send() if sent else copy.wait_recv()

    def exchange(phase, h):
        def send(to):
            remote(
                sbuf.at[phase, h, to],
                rbuf.at[phase, h, me],
                aa_s.at[phase, h],
                aa_r.at[phase, h],
                to,
                gx,
            ).start()

        each_partner(send)
        rbuf[phase, h, me] = sbuf[phase, h, me]

    def exchange_sync(phase, h, sent):
        view = (sbuf if sent else rbuf).at[phase, h, pl.ds(0, others)]
        to = lax.rem(me + 1, owners)
        copy = remote(view, view, aa_s.at[phase, h], aa_r.at[phase, h], to, gx)
        copy.wait_send() if sent else copy.wait_recv()

    def reduce_start(level, h):
        for step in FAR_FIRST:
            to = peer(step)
            remote(
                rs_s.at[level, h, :, pl.ds(pl.multiple_of(to * rows, rows), rows), :],
                rs_r.at[level, h, gx],
                rd_s.at[level, h],
                rd_r.at[level, h],
                me,
                to,
            ).start()

    def reduce_sync(level, h, sent):
        view = rs_r.at[level, h, pl.ds(0, groups - 1)]
        copy = remote(view, view, rd_s.at[level, h], rd_r.at[level, h], me, peer(1))
        copy.wait_send() if sent else copy.wait_recv()

    def hot(mask):
        return jnp.where(mask, 1.0, 0.0).astype(BF)

    def index_level(level):
        down = lax.broadcasted_iota(jnp.int32, (routed, routed), 0)
        across = lax.broadcasted_iota(jnp.int32, (routed, routed), 1)
        supernode = lax.div(down, group_rows)
        moved = across == (down - supernode * group_rows) * per + supernode

        def turn(mask, values, axis):
            return jnp.sum(jnp.where(mask, values, 0.0), axis=axis, keepdims=True)

        column = turn(moved, owner_in[level].astype(F32), 1)
        row = turn(down == across, column, 0)
        want = turn(down == across, turn(moved, target_in[level].astype(F32), 1), 0)
        row, column = row.astype(jnp.int32), column.astype(jnp.int32)
        want = want.astype(jnp.int32) + 1
        same = row == column
        rank_c = jnp.sum(jnp.where(same & (across < down), 1.0, 0.0), axis=1, keepdims=True)
        rank_r = jnp.sum(jnp.where(same & (down < across), 1.0, 0.0), axis=0, keepdims=True)
        rank_c, rank_r = rank_c.astype(jnp.int32), rank_r.astype(jnp.int32)
        pos_r[level] = row * cap + rank_r
        pos_c[level] = column * cap + rank_c
        owner = lax.broadcasted_iota(jnp.int32, (owners, routed), 0)
        high = lax.div(want, 32)
        low_bits = (want - high * 32).astype(F32)
        high = jnp.where(owner == row, high.astype(F32), 0.0).astype(BF)
        low_bits = jnp.where(owner == row, low_bits, 0.0).astype(BF)
        lane = lax.broadcasted_iota(jnp.int32, (routed, LANES), 1)
        place = hot(lane == rank_c + level * SLOT_LANES)
        chosen = dot(high, place) * 32.0 + dot(low_bits, place)
        pick[...] = chosen if level == 0 else pick[...] + chosen

    def build_p(level):
        for c in range(slots // LANES):
            at = lax.broadcasted_iota(jnp.int32, (LANES, routed), 0) + c * LANES
            pm[level, pl.ds(c * LANES, LANES), :] = hot(at == pos_r[level])

    def build_pt(level):
        for c in range(routed // LANES):
            span = pl.ds(c * LANES, LANES)
            at = lax.broadcasted_iota(jnp.int32, (LANES, slots), 1)
            pt[level, span, :] = hot(at == pos_c[level, span, :])

    def build_s(level):
        at = lax.broadcasted_iota(jnp.int32, (SLOT_LANES, slots), 0)
        span = pl.ds(pl.multiple_of(level * SLOT_LANES, SLOT_LANES), SLOT_LANES)
        lane = lax.broadcasted_iota(jnp.int32, (1, slots), 1)
        own = lane - lax.div(lane, cap) * cap
        row = jnp.sum(jnp.where(at == own, by_row[span, :], 0.0), axis=0, keepdims=True)
        row = row.astype(jnp.int32)
        for c in range(sends * block // LANES):
            at = lax.broadcasted_iota(jnp.int32, (LANES, slots), 0) + (c * LANES + block + 1)
            sm[level, pl.ds(c * LANES, LANES), :] = hot(at == row)

    def build_g(level):
        for c in range(slots // LANES):
            span = pl.ds(c * LANES, LANES)
            lane = lax.broadcasted_iota(jnp.int32, (LANES, LANES), 1)
            order = lax.broadcasted_iota(jnp.int32, (LANES, 1), 0) + c * LANES
            own = order - lax.div(order, cap) * cap + level * SLOT_LANES
            column = jnp.sum(jnp.where(lane == own, by_col[span, :], 0.0), axis=1, keepdims=True)
            at = lax.broadcasted_iota(jnp.int32, (LANES, sends * block), 1) + (block + 1)
            gm[level, span, :] = hot(at == column.astype(jnp.int32))

    def spread():
        number = told[...].reshape(owners, LANES)
        high = lax.div(number, 32)
        low_bits = (number - high * 32).astype(F32).astype(BF)
        high = high.astype(F32).astype(BF)
        first = lax.broadcasted_iota(jnp.int32, (slots, owners), 0)
        owner = lax.broadcasted_iota(jnp.int32, (slots, owners), 1) * cap
        fan = hot((first >= owner) & (first < owner + cap))
        by_col[...] = dot(fan, high) * 32.0 + dot(fan, low_bits)
        first = lax.broadcasted_iota(jnp.int32, (owners, slots), 1)
        owner = lax.broadcasted_iota(jnp.int32, (owners, slots), 0) * cap
        fan = hot((first >= owner) & (first < owner + cap))
        by_row[...] = dot_t(high, fan) * 32.0 + dot_t(low_bits, fan)

    def pack(phase, h, value):
        sbuf[phase, h] = value.astype(BF).reshape(owners, cap // 2, 2, LANES)

    def unpack(phase, h):
        return rbuf[phase, h].reshape(slots, LANES)

    loads[0].wait()
    for h in range(halves):
        blk[0, h, :, my_rows, :] = rhs[0, :, :, h * LANES : (h + 1) * LANES]
    for level in range(sends):
        index_level(level)
    asked[...] = pick[...].astype(jnp.int32).reshape(owners, 1, LANES)
    told[me] = asked[me]
    pl.semaphore_wait(barrier, others + groups - 1)
    gather(0, 0)
    matrix(0, finv, fwd_inv, fs, fr)
    columns(0)
    for h in range(1, halves):
        gather(0, h)

    def tell(to):
        remote(asked.at[to], told.at[me], ix_s, ix_r, to, gx).start()

    each_partner(tell)
    for level in range(levels):
        if level > 0:
            for h in range(halves):
                acc[level, h] = (
                    rhs[level, :, :, h * LANES : (h + 1) * LANES].astype(F32).reshape(block, LANES)
                )
    for level in range(sends):
        build_p(level)
    first = told.at[pl.ds(0, others)]
    remote(first, first, ix_s, ix_r, lax.rem(me + 1, owners), gx).wait_recv()
    spread()
    for load in loads[1:]:
        load.wait()

    def lower(level, h):
        matrix_waited = []
        for k in range(per):
            solved = dot(finv[level, k], blk[level, h, k])
            low[h, k] = solved.astype(BF)
            matrix_waited.append(low[h, k])
        return matrix_waited

    def forward(level, c):
        matrix_sync(level, finv, fs, fr, False)
        view = part(ucol.at[level], width - rows)
        remote(view, view, us.at[level], ur.at[level], me, peer(1)).wait_recv()
        for h in range(halves):
            gather_sync(level, h, False)
            lowered = lower(level, h)
            summed = [dot_t(ucol[level, k], lowered[k]).astype(BF) for k in range(per)]
            packed = dot(pm[level], jnp.concatenate(summed, axis=0))
            pack(level, h, packed)
            exchange(level, h)
        matrix(level + 1, finv, fwd_inv, fs, fr)

        @pl.when(level < sends - 1)
        def _():
            columns(level + 1)

        @pl.when(level == sends - 1)
        def _():
            matrix(sends - 1, binv, bwd_in, bs, br)

        build_s(level)
        build_g(level)
        build_pt(level)
        for h in range(halves):
            for k in range(per):
                const[level, h, k] = dot(bwd_inv[level, k], low[h, k])
        for h in range(halves):
            exchange_sync(level, h, False)
            come = unpack(level, h)
            chosen = sm[level, pl.ds(pl.multiple_of(level * block, block), block), :]
            total = acc[level + 1, h] - dot(chosen, come)
            blk[level + 1, h, :, my_rows, :] = total.astype(BF).reshape(per, rows, LANES)
            gather(level + 1, h)
        for h in range(halves):
            come = unpack(level, h)

            def later(target, c, h=h, come=come):
                span = pl.ds(pl.multiple_of((target - 1) * block, block), block)
                acc[target, h] = acc[target, h] - dot(sm[level, span, :], come)
                return c

            lax.fori_loop(level + 2, levels, later, 0)
        return c

    lax.fori_loop(0, sends, forward, 0)

    def finish(level, h, k, value):
        result = value.astype(BF)
        at = level * block + k * rows
        if not isinstance(at, int):
            at = pl.multiple_of(at, rows)
        sol[h, pl.ds(at, rows), :] = result
        out[level, k, :, h * LANES : (h + 1) * LANES] = result

    def leave(level):
        return pltpu.make_async_copy(out.at[level], out_far.at[level], out_sem.at[level])

    sol[...] = jnp.zeros(sol.shape, BF)
    matrix_sync(sends, finv, fs, fr, False)
    for h in range(halves):
        gather_sync(sends, h, False)
        lowered = lower(sends, h)
        for k in range(per):
            finish(sends, h, k, dot(bwd_inv[sends, k], lowered[k]))
    leave(sends).start()

    def backward(i, c):
        level = sends - 1 - i
        phase = sends + level
        for h in range(halves):
            answer = dot(gm[level], sol[h, pl.ds(block, sends * block), :])
            pack(phase, h, answer)
            exchange(phase, h)

        @pl.when(level > 0)
        def _():
            matrix(level - 1, binv, bwd_in, bs, br)

        matrix_sync(level, binv, bs, br, False)
        for h in range(halves):
            exchange_sync(phase, h, False)
            pulled = dot(pt[level], unpack(phase, h)).astype(BF)
            for k in range(per):
                upper = dot_t(bwd[level, k], pulled[k * group_rows : (k + 1) * group_rows])
                rs_s[level, h, k] = dot(binv[level, k], upper.astype(BF)).astype(BF)
            reduce_start(level, h)
        for h in range(halves):
            reduce_sync(level, h, False)
            for k in range(per):
                total = rs_s[level, h, k, my_rows, :].astype(F32)
                for step in range(1, groups):
                    total = total + rs_r[level, h, peer(step), k].astype(F32)
                finish(level, h, k, const[level, h, k] - total)
        leave(level).start()
        return c

    lax.fori_loop(0, sends, backward, 0)

    def drain(level, c):
        matrix_sync(level, finv, fs, fr, True)
        for h in range(halves):
            gather_sync(level, h, True)
        leave(level).wait()
        return c

    lax.fori_loop(0, levels, drain, 0)
    remote(first, first, ix_s, ix_r, lax.rem(me + 1, owners), gx).wait_send()

    def drain_sends(level, c):
        matrix_sync(level, binv, bs, br, True)
        view = part(ucol.at[level], width - rows)
        remote(view, view, us.at[level], ur.at[level], me, peer(1)).wait_send()
        for h in range(halves):
            exchange_sync(level, h, True)
            exchange_sync(level + sends, h, True)
            reduce_sync(level, h, True)
        return c

    lax.fori_loop(0, sends, drain_sends, 0)


def local(rhs, fwd_inv, bwd_inv, upd_t, bwd_t, dest_owner, dest_row):
    levels, per, rows, cols = rhs.shape
    group_rows = bwd_t.shape[2]
    owners = lax.axis_size("leaf")
    groups = lax.axis_size("grid")
    cap = max(2, 8 * per * group_rows // (3 * owners))
    sends = levels - 1
    halves = cols // LANES
    slots = owners * cap
    routed = per * group_rows
    block = per * rows
    width = rows * groups

    dma = pltpu.SemaphoreType.DMA
    vmem = pltpu.VMEM
    sizes = (levels, per, rows, group_rows, owners, groups, cap, halves)

    def body(*refs):
        solve_kernel(sizes, *refs)

    return pl.pallas_call(
        body,
        out_shape=jax.ShapeDtypeStruct(rhs.shape, BF),
        in_specs=[pl.BlockSpec(memory_space=pl.ANY)] * 5
        + [pl.BlockSpec(memory_space=vmem)] * 2,
        out_specs=pl.BlockSpec(memory_space=pl.ANY),
        scratch_shapes=[
            vmem((levels, per, width, width), BF),
            vmem((sends, per, width, width), BF),
            vmem((sends, per, width, group_rows), BF),
            vmem((levels, halves, per, width, LANES), BF),
            vmem((halves, per, width, LANES), BF),
            vmem((levels, halves, block, LANES), F32),
            vmem((sends, halves, per, rows, LANES), F32),
            vmem((halves, levels * block, LANES), BF),
            vmem((2 * sends, halves, owners, cap // 2, 2, LANES), BF),
            vmem((2 * sends, halves, owners, cap // 2, 2, LANES), BF),
            vmem((sends, halves, per, width, LANES), BF),
            vmem((sends, halves, groups, per, rows, LANES), BF),
            vmem((sends, slots, routed), BF),
            vmem((sends, routed, slots), BF),
            vmem((sends, sends * block, slots), BF),
            vmem((sends, slots, sends * block), BF),
            vmem((owners, 1, LANES), jnp.int32),
            vmem((LANES, slots), F32),
            vmem((slots, LANES), F32),
            vmem((owners, 1, LANES), jnp.int32),
            vmem((owners, LANES), F32),
            vmem((sends, 1, routed), jnp.int32),
            vmem((sends, routed, 1), jnp.int32),
            dma((levels,)),
            dma((levels,)),
            dma((sends,)),
            dma((sends,)),
            dma((sends,)),
            dma((sends,)),
            dma((levels, halves)),
            dma((levels, halves)),
            dma((2 * sends, halves)),
            dma((2 * sends, halves)),
            dma((sends, halves)),
            dma((sends, halves)),
            dma,
            dma,
            vmem(rhs.shape, BF),
            vmem(bwd_inv.shape, BF),
            vmem(bwd_t.shape, BF),
            vmem(rhs.shape, BF),
            dma((6,)),
            dma((levels,)),
        ],
        compiler_params=pltpu.CompilerParams(collective_id=0, has_side_effects=True),
    )(
        rhs,
        fwd_inv,
        bwd_inv,
        upd_t,
        bwd_t,
        dest_owner.reshape(sends, 1, routed),
        dest_row.reshape(sends, 1, routed),
    )


def solution(mesh):
    placed = (
        P(None, "leaf", "grid", None),
        P(None, "leaf", "grid", None),
        P(None, "leaf", "grid", None),
        P(None, "leaf", "grid", None),
        P(None, "leaf", "grid", None),
        P(None, "leaf", "grid", None, None),
        P(None, "leaf", "grid", None),
    )
    return jax.shard_map(
        local, mesh=mesh, in_specs=placed, out_specs=P(None, "leaf", "grid", None), check_vma=False
    )
```

```python
import jax
import jax.numpy as jnp
from jax import lax
from jax.experimental import pallas as pl
from jax.experimental.pallas import tpu as pltpu
from jax.sharding import PartitionSpec as P

MESH = pl.DeviceIdType.MESH
BF = jnp.bfloat16
F32 = jnp.float32
LANES = 128
RING_Y, RING_Z, CORES = 4, 8, 2
SLOT_LANES = 16
FAR_FIRST = (2, 1, 3)


def dot(a, b):
    return jnp.dot(a, b, preferred_element_type=F32)


def dot_t(a, b):
    return lax.dot_general(a, b, (((0,), (0,)), ((), ())), preferred_element_type=F32)


def count_out(place, count):
    return count // 2 + (place + 1) // 2 * (1 - 2 * (place % 2))


def solve_kernel(
    sizes,
    rhs_in,
    fwd_inv,
    bwd_in,
    upd,
    bwd_far,
    owner_in,
    target_in,
    out_far,
    finv,
    binv,
    ucol,
    blk,
    low,
    acc,
    const,
    sol,
    sbuf,
    rbuf,
    rs_s,
    rs_r,
    pm,
    pt,
    sm,
    gm,
    told,
    by_row,
    by_col,
    asked,
    pick,
    pos_r,
    pos_c,
    fs,
    fr,
    us,
    ur,
    bs,
    br,
    ag_s,
    ag_r,
    aa_s,
    aa_r,
    rd_s,
    rd_r,
    ix_s,
    ix_r,
    rhs,
    bwd_inv,
    bwd,
    out,
    in_sem,
    out_sem,
):
    levels, per, rows, group_rows, owners, groups, cap, halves = sizes
    sends = levels - 1
    width = rows * groups
    block = per * rows
    slots = owners * cap
    routed = per * group_rows
    me = lax.axis_index("leaf")
    gx = lax.axis_index("grid")
    my_rows = pl.ds(pl.multiple_of(gx * rows, rows), rows)
    others = owners - 1
    my_y = lax.div(me, RING_Z * CORES)
    my_z = lax.rem(lax.div(me, CORES), RING_Z)
    my_core = lax.rem(me, CORES)

    def peer(step):
        return lax.rem(gx + step, groups)

    def outward(place, count):
        half = lax.div(place + 1, 2)
        return count // 2 + half * (1 - 2 * lax.rem(place, 2))

    ring = [
        lax.rem(my_z + count_out(a, RING_Z), RING_Z) * CORES for a in range(RING_Z)
    ]

    def each_partner(act):
        def group(j, last):
            y = lax.rem(my_y + outward(lax.rem(j, RING_Y), RING_Y), RING_Y)
            core = lax.rem(my_core + 1 - lax.div(j, RING_Y), CORES)
            base = y * (RING_Z * CORES) + core
            for a in range(RING_Z - last):
                act(base + ring[a])

        def body(j, c):
            group(j, 0)
            return c

        lax.fori_loop(0, RING_Y * CORES - 1, body, 0)
        group(jnp.int32(RING_Y * CORES - 1), 1)

    def remote(src, dst, send, recv, leaf, grid):
        return pltpu.make_async_remote_copy(
            src_ref=src,
            dst_ref=dst,
            send_sem=send,
            recv_sem=recv,
            device_id=(leaf, grid),
            device_id_type=MESH,
        )

    barrier = pltpu.get_barrier_semaphore()

    def greet(to):
        pl.semaphore_signal(barrier, inc=1, device_id=(to, gx), device_id_type=MESH)

    each_partner(greet)
    for step in range(1, groups):
        pl.semaphore_signal(barrier, inc=1, device_id=(me, peer(step)), device_id_type=MESH)

    my_columns = pl.ds(pl.multiple_of(gx * group_rows, group_rows), group_rows)
    loads = [
        pltpu.make_async_copy(rhs_in, rhs, in_sem.at[0]),
        pltpu.make_async_copy(bwd_in, bwd_inv, in_sem.at[1]),
        pltpu.make_async_copy(bwd_far, bwd, in_sem.at[2]),
        pltpu.make_async_copy(fwd_inv, finv.at[:, :, my_rows, :], in_sem.at[3]),
        pltpu.make_async_copy(
            bwd_in.at[pl.ds(0, sends)], binv.at[:, :, my_rows, :], in_sem.at[4]
        ),
        pltpu.make_async_copy(
            upd.at[:, :, :, my_columns], ucol.at[:, :, my_rows, :], in_sem.at[5]
        ),
    ]
    for load in loads:
        load.start()

    def part(ref, count):
        return ref.at[:, pl.ds(0, count), :]

    def matrix(level, ref, mine, send, recv):
        for step in FAR_FIRST:
            remote(
                mine.at[level],
                ref.at[level, :, my_rows, :],
                send.at[level],
                recv.at[level],
                me,
                peer(step),
            ).start()

    def matrix_sync(level, ref, send, recv, sent):
        view = part(ref.at[level], width - rows)
        copy = remote(view, view, send.at[level], recv.at[level], me, peer(1))
        copy.wait_send() if sent else copy.wait_recv()

    def columns(level):
        for step in FAR_FIRST:
            to = peer(step)
            remote(
                upd.at[level, :, :, pl.ds(pl.multiple_of(to * group_rows, group_rows), group_rows)],
                ucol.at[level, :, my_rows, :],
                us.at[level],
                ur.at[level],
                me,
                to,
            ).start()

    def gather(level, h):
        view = blk.at[level, h, :, my_rows, :]
        for step in FAR_FIRST:
            remote(view, view, ag_s.at[level, h], ag_r.at[level, h], me, peer(step)).start()

    def gather_sync(level, h, sent):
        view = part(blk.at[level, h], width - rows)
        copy = remote(view, view, ag_s.at[level, h], ag_r.at[level, h], me, peer(1))
        copy.wait_send() if sent else copy.wait_recv()

    def exchange(phase, h):
        def send(to):
            remote(
                sbuf.at[phase, h, to],
                rbuf.at[phase, h, me],
                aa_s.at[phase, h],
                aa_r.at[phase, h],
                to,
                gx,
            ).start()

        each_partner(send)
        rbuf[phase, h, me] = sbuf[phase, h, me]

    def exchange_sync(phase, h, sent):
        view = (sbuf if sent else rbuf).at[phase, h, pl.ds(0, others)]
        to = lax.rem(me + 1, owners)
        copy = remote(view, view, aa_s.at[phase, h], aa_r.at[phase, h], to, gx)
        copy.wait_send() if sent else copy.wait_recv()

    def reduce_start(level, h):
        for step in FAR_FIRST:
            to = peer(step)
            remote(
                rs_s.at[level, h, :, pl.ds(pl.multiple_of(to * rows, rows), rows), :],
                rs_r.at[level, h, gx],
                rd_s.at[level, h],
                rd_r.at[level, h],
                me,
                to,
            ).start()

    def reduce_sync(level, h, sent):
        view = rs_r.at[level, h, pl.ds(0, groups - 1)]
        copy = remote(view, view, rd_s.at[level, h], rd_r.at[level, h], me, peer(1))
        copy.wait_send() if sent else copy.wait_recv()

    def hot(mask):
        return jnp.where(mask, 1.0, 0.0).astype(BF)

    def index_level(level):
        down = lax.broadcasted_iota(jnp.int32, (routed, routed), 0)
        across = lax.broadcasted_iota(jnp.int32, (routed, routed), 1)
        supernode = lax.div(down, group_rows)
        moved = across == (down - supernode * group_rows) * per + supernode

        def turn(mask, values, axis):
            return jnp.sum(jnp.where(mask, values, 0.0), axis=axis, keepdims=True)

        column = turn(moved, owner_in[level].astype(F32), 1)
        row = turn(down == across, column, 0)
        want = turn(down == across, turn(moved, target_in[level].astype(F32), 1), 0)
        row, column = row.astype(jnp.int32), column.astype(jnp.int32)
        want = want.astype(jnp.int32) + 1
        same = row == column
        rank_c = jnp.sum(jnp.where(same & (across < down), 1.0, 0.0), axis=1, keepdims=True)
        rank_r = jnp.sum(jnp.where(same & (down < across), 1.0, 0.0), axis=0, keepdims=True)
        rank_c, rank_r = rank_c.astype(jnp.int32), rank_r.astype(jnp.int32)
        pos_r[level] = row * cap + rank_r
        pos_c[level] = column * cap + rank_c
        owner = lax.broadcasted_iota(jnp.int32, (owners, routed), 0)
        high = lax.div(want, 32)
        low_bits = (want - high * 32).astype(F32)
        high = jnp.where(owner == row, high.astype(F32), 0.0).astype(BF)
        low_bits = jnp.where(owner == row, low_bits, 0.0).astype(BF)
        lane = lax.broadcasted_iota(jnp.int32, (routed, LANES), 1)
        place = hot(lane == rank_c + level * SLOT_LANES)
        chosen = dot(high, place) * 32.0 + dot(low_bits, place)
        pick[...] = chosen if level == 0 else pick[...] + chosen

    def build_p(level):
        for c in range(slots // LANES):
            at = lax.broadcasted_iota(jnp.int32, (LANES, routed), 0) + c * LANES
            pm[level, pl.ds(c * LANES, LANES), :] = hot(at == pos_r[level])

    def build_pt(level):
        for c in range(routed // LANES):
            span = pl.ds(c * LANES, LANES)
            at = lax.broadcasted_iota(jnp.int32, (LANES, slots), 1)
            pt[level, span, :] = hot(at == pos_c[level, span, :])

    def build_s(level):
        at = lax.broadcasted_iota(jnp.int32, (SLOT_LANES, slots), 0)
        span = pl.ds(pl.multiple_of(level * SLOT_LANES, SLOT_LANES), SLOT_LANES)
        lane = lax.broadcasted_iota(jnp.int32, (1, slots), 1)
        own = lane - lax.div(lane, cap) * cap
        row = jnp.sum(jnp.where(at == own, by_row[span, :], 0.0), axis=0, keepdims=True)
        row = row.astype(jnp.int32)
        for c in range(sends * block // LANES):
            at = lax.broadcasted_iota(jnp.int32, (LANES, slots), 0) + (c * LANES + block + 1)
            sm[level, pl.ds(c * LANES, LANES), :] = hot(at == row)

    def build_g(level):
        for c in range(slots // LANES):
            span = pl.ds(c * LANES, LANES)
            lane = lax.broadcasted_iota(jnp.int32, (LANES, LANES), 1)
            order = lax.broadcasted_iota(jnp.int32, (LANES, 1), 0) + c * LANES
            own = order - lax.div(order, cap) * cap + level * SLOT_LANES
            column = jnp.sum(jnp.where(lane == own, by_col[span, :], 0.0), axis=1, keepdims=True)
            at = lax.broadcasted_iota(jnp.int32, (LANES, sends * block), 1) + (block + 1)
            gm[level, span, :] = hot(at == column.astype(jnp.int32))

    def spread():
        number = told[...].reshape(owners, LANES)
        high = lax.div(number, 32)
        low_bits = (number - high * 32).astype(F32).astype(BF)
        high = high.astype(F32).astype(BF)
        first = lax.broadcasted_iota(jnp.int32, (slots, owners), 0)
        owner = lax.broadcasted_iota(jnp.int32, (slots, owners), 1) * cap
        fan = hot((first >= owner) & (first < owner + cap))
        by_col[...] = dot(fan, high) * 32.0 + dot(fan, low_bits)
        first = lax.broadcasted_iota(jnp.int32, (owners, slots), 1)
        owner = lax.broadcasted_iota(jnp.int32, (owners, slots), 0) * cap
        fan = hot((first >= owner) & (first < owner + cap))
        by_row[...] = dot_t(high, fan) * 32.0 + dot_t(low_bits, fan)

    def pack(phase, h, value):
        sbuf[phase, h] = value.astype(BF).reshape(owners, cap // 2, 2, LANES)

    def unpack(phase, h):
        return rbuf[phase, h].reshape(slots, LANES)

    loads[0].wait()
    for h in range(halves):
        blk[0, h, :, my_rows, :] = rhs[0, :, :, h * LANES : (h + 1) * LANES]
    for level in range(sends):
        index_level(level)
    asked[...] = pick[...].astype(jnp.int32).reshape(owners, 1, LANES)
    told[me] = asked[me]
    pl.semaphore_wait(barrier, others + groups - 1)
    gather(0, 0)
    matrix(0, finv, fwd_inv, fs, fr)
    columns(0)
    for h in range(1, halves):
        gather(0, h)

    def tell(to):
        remote(asked.at[to], told.at[me], ix_s, ix_r, to, gx).start()

    each_partner(tell)
    for level in range(levels):
        if level > 0:
            for h in range(halves):
                acc[level, h] = (
                    rhs[level, :, :, h * LANES : (h + 1) * LANES].astype(F32).reshape(block, LANES)
                )
    for level in range(sends):
        build_p(level)
    first = told.at[pl.ds(0, others)]
    remote(first, first, ix_s, ix_r, lax.rem(me + 1, owners), gx).wait_recv()
    spread()
    for load in loads[1:]:
        load.wait()

    def lower(level, h):
        matrix_waited = []
        for k in range(per):
            solved = dot(finv[level, k], blk[level, h, k])
            low[h, k] = solved.astype(BF)
            matrix_waited.append(low[h, k])
        return matrix_waited

    def forward(level, c):
        matrix_sync(level, finv, fs, fr, False)
        view = part(ucol.at[level], width - rows)
        remote(view, view, us.at[level], ur.at[level], me, peer(1)).wait_recv()
        for h in range(halves):
            gather_sync(level, h, False)
            lowered = lower(level, h)
            summed = [dot_t(ucol[level, k], lowered[k]).astype(BF) for k in range(per)]
            packed = dot(pm[level], jnp.concatenate(summed, axis=0))
            pack(level, h, packed)
            exchange(level, h)
            if h == 0:
                matrix(level + 1, finv, fwd_inv, fs, fr)

        @pl.when(level < sends - 1)
        def _():
            columns(level + 1)

        @pl.when(level == sends - 1)
        def _():
            matrix(sends - 1, binv, bwd_in, bs, br)

        build_s(level)
        build_g(level)
        build_pt(level)
        for h in range(halves):
            for k in range(per):
                const[level, h, k] = dot(bwd_inv[level, k], low[h, k])
        for h in range(halves):
            exchange_sync(level, h, False)
            come = unpack(level, h)
            chosen = sm[level, pl.ds(pl.multiple_of(level * block, block), block), :]
            total = acc[level + 1, h] - dot(chosen, come)
            blk[level + 1, h, :, my_rows, :] = total.astype(BF).reshape(per, rows, LANES)
            gather(level + 1, h)
        for h in range(halves):
            come = unpack(level, h)

            def later(target, c, h=h, come=come):
                span = pl.ds(pl.multiple_of((target - 1) * block, block), block)
                acc[target, h] = acc[target, h] - dot(sm[level, span, :], come)
                return c

            lax.fori_loop(level + 2, levels, later, 0)
        return c

    lax.fori_loop(0, sends, forward, 0)

    def finish(level, h, k, value):
        result = value.astype(BF)
        at = level * block + k * rows
        if not isinstance(at, int):
            at = pl.multiple_of(at, rows)
        sol[h, pl.ds(at, rows), :] = result
        out[level, k, :, h * LANES : (h + 1) * LANES] = result

    def leave(level):
        return pltpu.make_async_copy(out.at[level], out_far.at[level], out_sem.at[level])

    sol[...] = jnp.zeros(sol.shape, BF)
    matrix_sync(sends, finv, fs, fr, False)
    for h in range(halves):
        gather_sync(sends, h, False)
        lowered = lower(sends, h)
        for k in range(per):
            finish(sends, h, k, dot(bwd_inv[sends, k], lowered[k]))
    leave(sends).start()

    def backward(i, c):
        level = sends - 1 - i
        phase = sends + level
        for h in range(halves):
            answer = dot(gm[level], sol[h, pl.ds(block, sends * block), :])
            pack(phase, h, answer)
            exchange(phase, h)

        @pl.when(level > 0)
        def _():
            matrix(level - 1, binv, bwd_in, bs, br)

        matrix_sync(level, binv, bs, br, False)
        for h in range(halves):
            exchange_sync(phase, h, False)
            pulled = dot(pt[level], unpack(phase, h)).astype(BF)
            for k in range(per):
                upper = dot_t(bwd[level, k], pulled[k * group_rows : (k + 1) * group_rows])
                rs_s[level, h, k] = dot(binv[level, k], upper.astype(BF)).astype(BF)
            reduce_start(level, h)
        for h in range(halves):
            reduce_sync(level, h, False)
            for k in range(per):
                total = rs_s[level, h, k, my_rows, :].astype(F32)
                for step in range(1, groups):
                    total = total + rs_r[level, h, peer(step), k].astype(F32)
                finish(level, h, k, const[level, h, k] - total)
        leave(level).start()
        return c

    lax.fori_loop(0, sends, backward, 0)

    def drain(level, c):
        matrix_sync(level, finv, fs, fr, True)
        for h in range(halves):
            gather_sync(level, h, True)
        leave(level).wait()
        return c

    lax.fori_loop(0, levels, drain, 0)
    remote(first, first, ix_s, ix_r, lax.rem(me + 1, owners), gx).wait_send()

    def drain_sends(level, c):
        matrix_sync(level, binv, bs, br, True)
        view = part(ucol.at[level], width - rows)
        remote(view, view, us.at[level], ur.at[level], me, peer(1)).wait_send()
        for h in range(halves):
            exchange_sync(level, h, True)
            exchange_sync(level + sends, h, True)
            reduce_sync(level, h, True)
        return c

    lax.fori_loop(0, sends, drain_sends, 0)


def local(rhs, fwd_inv, bwd_inv, upd_t, bwd_t, dest_owner, dest_row):
    levels, per, rows, cols = rhs.shape
    group_rows = bwd_t.shape[2]
    owners = lax.axis_size("leaf")
    groups = lax.axis_size("grid")
    cap = max(2, 8 * per * group_rows // (3 * owners))
    sends = levels - 1
    halves = cols // LANES
    slots = owners * cap
    routed = per * group_rows
    block = per * rows
    width = rows * groups

    dma = pltpu.SemaphoreType.DMA
    vmem = pltpu.VMEM
    sizes = (levels, per, rows, group_rows, owners, groups, cap, halves)

    def body(*refs):
        solve_kernel(sizes, *refs)

    return pl.pallas_call(
        body,
        out_shape=jax.ShapeDtypeStruct(rhs.shape, BF),
        in_specs=[pl.BlockSpec(memory_space=pl.ANY)] * 5
        + [pl.BlockSpec(memory_space=vmem)] * 2,
        out_specs=pl.BlockSpec(memory_space=pl.ANY),
        scratch_shapes=[
            vmem((levels, per, width, width), BF),
            vmem((sends, per, width, width), BF),
            vmem((sends, per, width, group_rows), BF),
            vmem((levels, halves, per, width, LANES), BF),
            vmem((halves, per, width, LANES), BF),
            vmem((levels, halves, block, LANES), F32),
            vmem((sends, halves, per, rows, LANES), F32),
            vmem((halves, levels * block, LANES), BF),
            vmem((2 * sends, halves, owners, cap // 2, 2, LANES), BF),
            vmem((2 * sends, halves, owners, cap // 2, 2, LANES), BF),
            vmem((sends, halves, per, width, LANES), BF),
            vmem((sends, halves, groups, per, rows, LANES), BF),
            vmem((sends, slots, routed), BF),
            vmem((sends, routed, slots), BF),
            vmem((sends, sends * block, slots), BF),
            vmem((sends, slots, sends * block), BF),
            vmem((owners, 1, LANES), jnp.int32),
            vmem((LANES, slots), F32),
            vmem((slots, LANES), F32),
            vmem((owners, 1, LANES), jnp.int32),
            vmem((owners, LANES), F32),
            vmem((sends, 1, routed), jnp.int32),
            vmem((sends, routed, 1), jnp.int32),
            dma((levels,)),
            dma((levels,)),
            dma((sends,)),
            dma((sends,)),
            dma((sends,)),
            dma((sends,)),
            dma((levels, halves)),
            dma((levels, halves)),
            dma((2 * sends, halves)),
            dma((2 * sends, halves)),
            dma((sends, halves)),
            dma((sends, halves)),
            dma,
            dma,
            vmem(rhs.shape, BF),
            vmem(bwd_inv.shape, BF),
            vmem(bwd_t.shape, BF),
            vmem(rhs.shape, BF),
            dma((6,)),
            dma((levels,)),
        ],
        compiler_params=pltpu.CompilerParams(collective_id=0, has_side_effects=True),
    )(
        rhs,
        fwd_inv,
        bwd_inv,
        upd_t,
        bwd_t,
        dest_owner.reshape(sends, 1, routed),
        dest_row.reshape(sends, 1, routed),
    )


def solution(mesh):
    placed = (
        P(None, "leaf", "grid", None),
        P(None, "leaf", "grid", None),
        P(None, "leaf", "grid", None),
        P(None, "leaf", "grid", None),
        P(None, "leaf", "grid", None),
        P(None, "leaf", "grid", None, None),
        P(None, "leaf", "grid", None),
    )
    return jax.shard_map(
        local, mesh=mesh, in_specs=placed, out_specs=P(None, "leaf", "grid", None), check_vma=False
    )
```
